32 devices in a mesh: mem: 4 (over y, x), tile: 8 (over z, core).
Axes of the slice: x: 2, y: 2, z: 4, core: 2. Of those that a mesh axis runs over, the one named last changes fastest.
Arguments:
- members: float32 [40, 2, 65536], P('mem', None, 'tile'), may hold values from -6 to 6
- increment: float32 [2, 262144], P(None, 'tile'), may hold values from -6 to 6
- fine_angles: float32 [2, 262144], P(None, 'tile'), may hold values from -1.5 to 1.5
- coarse_angles: float32 [2, 65536], P(None, 'tile'), may hold values from -1.5 to 1.5
- remap_weights: bfloat16 [8, 64, 4, 256, 128], P('tile', 'mem'), may hold values from -0.1875 to 0.1875
- sources: int32 [8, 64, 4], P('tile', 'mem'), may hold values from 0 to 1023, as said below
- counts: int32 [8, 64], P('tile', 'mem'), may hold values from 2 to 4, as said below
Outputs:
- recentered: float32 [40, 2, 65536], P('mem', None, 'tile')
The draws below stay inside these ranges and needn't reach their ends.
Inputs may be any that keep to these rules, and one draw needn't show every extreme that they name: `sources`: for entry [s, l], with g = 64 s + l, slots 0 and 1 name fine blocks 2 g and 2 g + 1; each further even slot names block (2 g - r) mod 1024 and each further odd slot block (2 g + 1 + r + 512) mod 1024, each with its own r from 1 to 128. `counts`: every column shard holds a coarse block that uses all 4 slots.
All inputs are finite; a program needn't handle non-finite values.
Results may differ from the reference program's by a relative error of at most 0.0017.
Values may be sent and summed in bfloat16 or wider, within the bound.
A program may use at most 64 MiB of HBM per device.

```python
import jax
import jax.numpy as jnp
from jax import lax

BC = 128
BF = 256
KMAX = 4
MEMBERS = 40
CBT = 64
SHARDS = 8
NC = 65536
NFB = 1024
NF = 262144


def draw_sources(key, part):
    numbers = jnp.arange(SHARDS * CBT, dtype=jnp.int32).reshape(SHARDS, CBT, 1)
    reach = jax.random.randint(jax.random.fold_in(key, 11), (SHARDS, CBT, KMAX - 2), 1, 2 * CBT + 1, dtype=jnp.int32)
    sides = jnp.arange(KMAX - 2, dtype=jnp.int32) % 2
    below = jnp.mod(2 * numbers - reach, NFB)
    across = jnp.mod(2 * numbers + 1 + reach + NFB // 2, NFB)
    others = jnp.where(sides[None, None, :] == 0, below, across).astype(jnp.int32)
    return jnp.concatenate([2 * numbers, 2 * numbers + 1, others], axis=2).astype(jnp.int32)


def draw_counts(key, part):
    drawn = jax.random.randint(jax.random.fold_in(key, 7), (SHARDS, CBT), 2, KMAX + 1, dtype=jnp.int32)
    full_at = jax.random.randint(jax.random.fold_in(key, 8), (SHARDS, 1), 0, CBT, dtype=jnp.int32)
    positions = jnp.arange(CBT, dtype=jnp.int32)[None, :]
    return jnp.where(positions == full_at, KMAX, drawn).astype(jnp.int32)


def block_levels(key, shape, pieces, least, high):
    gain = 1.0
    for axis_at, blocks in pieces:
        draws = jax.random.uniform(jax.random.fold_in(jax.random.fold_in(key, 6), axis_at), (blocks,), jnp.float32, least / len(pieces), high / len(pieces))
        gain = gain * jnp.repeat(jnp.exp(draws), shape[axis_at] // blocks).reshape((-1,) + (1,) * (len(shape) - 1 - axis_at))
    return gain


def noise(key, shape, spread, most, shards=(), held_as=jnp.bfloat16):
    array = spread * jax.random.normal(key, shape, jnp.float32)
    if shards:
        array = array * block_levels(key, shape, shards, -0.22, 0.18)
    return jnp.clip(array, -most, most).astype(held_as)


def setup_inputs(seed: int = 0) -> dict:
    arg_keys = jax.random.split(jax.random.key(seed), 8)
    return {
        "members": noise(arg_keys[0], (MEMBERS, 2, NC), 1.0, 6.0, ((0, 4), (2, 8)), jnp.float32),
        "increment": noise(arg_keys[1], (2, NF), 1.0, 6.0, ((1, 8),), jnp.float32),
        "fine_angles": jnp.clip(jax.random.uniform(arg_keys[2], (2, NF), jnp.float32, -1.5, 1.5) * block_levels(arg_keys[2], (2, NF), ((1, 8),), -0.4, 0.0), -1.5, 1.5),
        "coarse_angles": jnp.clip(jax.random.uniform(arg_keys[3], (2, NC), jnp.float32, -1.5, 1.5) * block_levels(arg_keys[3], (2, NC), ((1, 8),), -0.4, 0.0), -1.5, 1.5),
        "remap_weights": noise(arg_keys[4], (SHARDS, CBT, KMAX, BF, BC), (KMAX * BF) ** -0.5, 0.1875, ((0, 8), (1, 4))),
        "sources": draw_sources(jax.random.fold_in(arg_keys[7], 71), 0),
        "counts": draw_counts(jax.random.fold_in(arg_keys[7], 71), 0),
    }


def to_vector(east_part, north_part, longitude, latitude):
    sin_lon, cos_lon = jnp.sin(longitude), jnp.cos(longitude)
    sin_lat, cos_lat = jnp.sin(latitude), jnp.cos(latitude)
    first = -sin_lon * east_part - sin_lat * cos_lon * north_part
    second = cos_lon * east_part - sin_lat * sin_lon * north_part
    third = cos_lat * north_part
    return first, second, third


def to_wind(first, second, third, longitude, latitude):
    sin_lon, cos_lon = jnp.sin(longitude), jnp.cos(longitude)
    sin_lat, cos_lat = jnp.sin(latitude), jnp.cos(latitude)
    east_part = -sin_lon * first + cos_lon * second
    north_part = -sin_lat * cos_lon * first - sin_lat * sin_lon * second + cos_lat * third
    return jnp.stack([east_part, north_part])


def reference(members, increment, fine_angles, coarse_angles, remap_weights, sources, counts):
    first, second, third = to_vector(increment[0], increment[1], fine_angles[0], fine_angles[1])
    fine_cart = jnp.stack([first, second, third]).astype(jnp.bfloat16)
    blocks = fine_cart.reshape(3, NFB, BF).transpose(1, 0, 2)

    def one_shard(shard_data):
        shard_weights, source_ids, slot_counts = shard_data
        picked = blocks[source_ids]
        live_slots = jnp.arange(KMAX, dtype=jnp.int32)[None, :] < slot_counts[:, None]
        picked = jnp.where(live_slots[:, :, None, None], picked, 0)
        return jnp.einsum('ikcf,ikfb->cib', picked.astype(jnp.float32), shard_weights.astype(jnp.float32))

    coarse = lax.map(one_shard, (remap_weights, sources, counts))
    coarse_cart = coarse.transpose(1, 0, 2, 3).reshape(3, NC)
    coarse_wind = to_wind(coarse_cart[0], coarse_cart[1], coarse_cart[2], coarse_angles[0], coarse_angles[1])
    member_mean = jnp.sum(members, axis=0) / MEMBERS
    return members - member_mean[None] + coarse_wind[None]
```

```python
import functools

import jax
import jax.numpy as jnp
from jax import lax
from jax.experimental import pallas as pl
from jax.experimental.pallas import tpu as pltpu
from jax.sharding import PartitionSpec as P

LANES = 128
MESH = pl.DeviceIdType.MESH


def to_vector(east_part, north_part, longitude, latitude):
    sin_lon, cos_lon = (jnp.sin(longitude), jnp.cos(longitude))
    sin_lat, cos_lat = (jnp.sin(latitude), jnp.cos(latitude))
    first = -sin_lon * east_part - sin_lat * cos_lon * north_part
    second = cos_lon * east_part - sin_lat * sin_lon * north_part
    third = cos_lat * north_part
    return (first, second, third)


def to_wind(first, second, third, longitude, latitude):
    sin_lon, cos_lon = (jnp.sin(longitude), jnp.cos(longitude))
    sin_lat, cos_lat = (jnp.sin(latitude), jnp.cos(latitude))
    east_part = -sin_lon * first + cos_lon * second
    north_part = -sin_lat * cos_lon * first - sin_lat * sin_lon * second + cos_lat * third
    return (east_part, north_part)


def kernel(
    tiles, mems, blocks, slots, fine_blocks, fine_width, member_count,
    src_ref, cnt_ref, inc_hbm, ang_hbm, cang_hbm, mem_hbm, w_hbm,
    out_ref,
    inc_v, ang_v, cang_v, mem_v, w_v,
    cart, picked, req_out, req_in, rows_out, rows_in,
    part, part_in, delta,
    load_sem, w_sem, req_send, req_recv, rows_send, rows_recv,
    part_send, part_recv, delta_send, delta_recv,
):
    tile = lax.axis_index("tile")
    mem = lax.axis_index("mem")
    half = tiles // 2
    pairs = (slots - 2) // 2
    halves = fine_width // LANES
    own_rows = 2 * blocks
    wide = pairs * blocks

    loads = [
        pltpu.make_async_copy(inc_hbm, inc_v, load_sem.at[0]),
        pltpu.make_async_copy(ang_hbm, ang_v, load_sem.at[1]),
        pltpu.make_async_copy(
            cang_hbm.at[pl.ds(pl.multiple_of(mem * own_rows, own_rows), own_rows)], cang_v, load_sem.at[2]
        ),
        pltpu.make_async_copy(mem_hbm, mem_v, load_sem.at[3]),
    ]
    near_depth = 2 * fine_width
    near_load = pltpu.make_async_copy(
        w_hbm.at[:, pl.ds(0, near_depth)], w_v.at[:, pl.ds(0, near_depth)], w_sem.at[0]
    )
    far_depth = (slots - 2) * fine_width
    far_load = pltpu.make_async_copy(
        w_hbm.at[:, pl.ds(near_depth, far_depth)], w_v.at[:, pl.ds(near_depth, far_depth)], w_sem.at[1]
    )
    for load in loads:
        load.start()
    near_load.start()
    far_load.start()

    barrier = pltpu.get_barrier_semaphore()
    offsets = sorted({1, tiles - 1, half, tiles - half, half + 1, tiles - half - 1})
    for by in offsets:
        pl.semaphore_signal(
            barrier, inc=1, device_id=(mem, lax.rem(tile + by, tiles)), device_id_type=MESH
        )
    for by in range(1, mems):
        pl.semaphore_signal(
            barrier, inc=1, device_id=(lax.rem(mem + by, mems), tile), device_id_type=MESH
        )

    row = lax.broadcasted_iota(jnp.int32, (blocks, fine_blocks), 0)
    column = lax.broadcasted_iota(jnp.int32, (blocks, fine_blocks), 1)

    def ids_of(slot):
        ids = jnp.full((blocks, fine_blocks), -1, jnp.int32)
        for block in range(blocks):
            name = jnp.where(slot < cnt_ref[0, block], src_ref[slot, block], -1)
            ids = jnp.where(row == block, name, ids)
        return ids

    def pick(ids, shard):
        return jnp.where(column == ids - shard * fine_blocks, 1.0, 0.0).astype(jnp.bfloat16)

    lower = lax.rem(tile + tiles - 1, tiles)
    across = lax.rem(tile + half, tiles)
    beyond = lax.rem(tile + half + 1, tiles)
    own_picks = []
    for pair in range(pairs):
        below_ids = ids_of(2 + 2 * pair)
        across_ids = ids_of(3 + 2 * pair)
        at = slice(pair * blocks, (pair + 1) * blocks)
        req_out[0, at, :] = pick(below_ids, lower)
        req_out[1, at, :] = pick(across_ids, across)
        req_out[2, at, :] = pick(across_ids, beyond)
        own_picks.append(pick(below_ids, tile))
    pl.semaphore_wait(barrier, len(offsets) + mems - 1)

    asked = (lower, across, beyond)
    requests = []
    for flow in range(3):
        requests.append(
            pltpu.make_async_remote_copy(
                src_ref=req_out.at[flow], dst_ref=req_in.at[flow],
                send_sem=req_send.at[flow], recv_sem=req_recv.at[flow],
                device_id=(mem, asked[flow]), device_id_type=MESH,
            )
        )
        requests[-1].start()

    loads[0].wait()
    loads[1].wait()
    step = 32
    for start in range(0, fine_blocks, step):
        for part_at in range(halves):

            def taken(ref, component):
                first_row = start * 2 * halves + 2 * part_at + component
                return ref[pl.ds(first_row, step, stride=2 * halves), :]

            vector = to_vector(taken(inc_v, 0), taken(inc_v, 1), taken(ang_v, 0), taken(ang_v, 1))
            for component in range(3):
                left = component * fine_width + part_at * LANES
                cart[start : start + step, left : left + LANES] = vector[component].astype(jnp.bfloat16)

    served = (
        lax.rem(tile + 1, tiles),
        lax.rem(tile + tiles - half, tiles),
        lax.rem(tile + tiles - half - 1, tiles),
    )
    replies = []
    for flow in range(3):
        requests[flow].wait_recv()
        found = jnp.dot(req_in[flow], cart[...], preferred_element_type=jnp.float32).astype(jnp.bfloat16)
        for component in range(3):
            rows_out[flow, component * wide : (component + 1) * wide, :] = found[
                :, component * fine_width : (component + 1) * fine_width
            ]
        replies.append(
            pltpu.make_async_remote_copy(
                src_ref=rows_out.at[flow], dst_ref=rows_in.at[flow],
                send_sem=rows_send.at[flow], recv_sem=rows_recv.at[flow],
                device_id=(mem, served[flow]), device_id_type=MESH,
            )
        )
        replies[-1].start()

    loads[3].wait()
    part[...] = jnp.sum(mem_v[...], axis=0)
    sums = []
    for by in range(1, mems):
        peer = lax.rem(mem + by, mems)
        sums.append(
            pltpu.make_async_remote_copy(
                src_ref=part.at[pl.ds(pl.multiple_of(peer * own_rows, own_rows), own_rows)],
                dst_ref=part_in.at[by - 1],
                send_sem=part_send.at[by - 1], recv_sem=part_recv.at[by - 1],
                device_id=(peer, tile), device_id_type=MESH,
            )
        )
        sums[-1].start()

    local = jnp.concatenate([pick(ids_of(0), tile), pick(ids_of(1), tile)] + own_picks, axis=0)
    found = jnp.dot(local, cart[...], preferred_element_type=jnp.float32).astype(jnp.bfloat16)
    for order in range(2 + pairs):
        slot = order if order < 2 else 2 * order - 2
        for component in range(3):
            picked[
                component * blocks : (component + 1) * blocks, slot * fine_width : (slot + 1) * fine_width
            ] = found[
                order * blocks : (order + 1) * blocks, component * fine_width : (component + 1) * fine_width
            ]

    loads[2].wait()
    coarse_lon = cang_v[pl.ds(0, blocks, stride=2), :]
    coarse_lat = cang_v[pl.ds(1, blocks, stride=2), :]
    sin_lon, cos_lon = (jnp.sin(coarse_lon), jnp.cos(coarse_lon))
    sin_lat, cos_lat = (jnp.sin(coarse_lat), jnp.cos(coarse_lat))

    owner = lax.rem(lax.broadcasted_iota(jnp.int32, (3 * blocks, LANES), 0), blocks)

    def remap(left, depth):
        values = picked[:, left : left + depth]
        total = jnp.zeros((3 * blocks, LANES), jnp.float32)
        for block in range(blocks):
            product = jnp.dot(values, w_v[block, left : left + depth, :], preferred_element_type=jnp.float32)
            total = jnp.where(owner == block, product, total)
        return total

    near_load.wait()
    vector = remap(0, near_depth)

    for copy in sums:
        copy.wait_recv()
    mean = part[pl.ds(pl.multiple_of(mem * own_rows, own_rows), own_rows), :]
    for by in range(mems - 1):
        mean = mean + part_in[by]
    mean = mean / member_count

    far_load.wait()
    for flow in range(3):
        replies[flow].wait_recv()
    for pair in range(pairs):
        for component in range(3):
            rows = slice(component * blocks, (component + 1) * blocks)
            came = slice(component * wide + pair * blocks, component * wide + (pair + 1) * blocks)
            below_at = slice((2 + 2 * pair) * fine_width, (3 + 2 * pair) * fine_width)
            across_at = slice((3 + 2 * pair) * fine_width, (4 + 2 * pair) * fine_width)
            picked[rows, below_at] = picked[rows, below_at] + rows_in[0, came, :]
            picked[rows, across_at] = rows_in[1, came, :] + rows_in[2, came, :]
    vector = vector + remap(near_depth, far_depth)

    first, second, third = (vector[at * blocks : (at + 1) * blocks] for at in range(3))
    east = -sin_lon * first + cos_lon * second
    north = -sin_lat * cos_lon * first - sin_lat * sin_lon * second + cos_lat * third
    base = pl.multiple_of(mem * own_rows, own_rows)
    delta[pl.ds(base, blocks, stride=2), :] = east
    delta[pl.ds(base + 1, blocks, stride=2), :] = north
    mine = pl.ds(base, own_rows)
    delta[mine, :] = delta[mine, :] - mean
    shares = []
    for by in range(1, mems):
        shares.append(
            pltpu.make_async_remote_copy(
                src_ref=delta.at[mine], dst_ref=delta.at[mine],
                send_sem=delta_send.at[by - 1], recv_sem=delta_recv.at[by - 1],
                device_id=(lax.rem(mem + by, mems), tile), device_id_type=MESH,
            )
        )
        shares[-1].start()
    for copy in shares:
        copy.wait_recv()
    out_ref[...] = delta[...]
    for copy in requests + replies + sums + shares:
        copy.wait_send()


def interleaved(array):
    lead = array.shape[:-2]
    count = array.shape[-1] // LANES
    split = array.reshape(lead + (2, count, LANES))
    return jnp.swapaxes(split, -3, -2).reshape(lead + (2 * count, LANES))


def shards(members, increment, fine_angles, coarse_angles, remap_weights, sources, counts):
    weights = remap_weights[0]
    blocks, slots, fine_width, coarse_width = weights.shape
    fine_blocks = increment.shape[1] // fine_width
    tiles, mems = (lax.axis_size("tile"), lax.axis_size("mem"))
    pairs = (slots - 2) // 2
    weights = weights.reshape(blocks, slots * fine_width, coarse_width)
    columns = coarse_angles.shape[1]
    rows = 2 * columns // LANES
    fine_rows = 2 * increment.shape[1] // LANES
    group = members.shape[0]
    operands = (
        sources[0].T,
        counts,
        interleaved(increment),
        interleaved(fine_angles),
        interleaved(coarse_angles),
        interleaved(members),
        weights,
    )
    any_spec = pl.BlockSpec(memory_space=pl.ANY)
    smem_spec = pl.BlockSpec(memory_space=pltpu.SMEM)
    dma = pltpu.SemaphoreType.DMA
    others = mems - 1
    delta = pl.pallas_call(
        functools.partial(kernel, tiles, mems, blocks, slots, fine_blocks, fine_width, group * mems),
        out_shape=jax.ShapeDtypeStruct((rows, LANES), jnp.float32),
        in_specs=[smem_spec, smem_spec] + [any_spec] * 5,
        out_specs=pl.BlockSpec(memory_space=pltpu.VMEM),
        scratch_shapes=[
            pltpu.VMEM((fine_rows, LANES), jnp.float32),
            pltpu.VMEM((fine_rows, LANES), jnp.float32),
            pltpu.VMEM((2 * blocks, LANES), jnp.float32),
            pltpu.VMEM((group, rows, LANES), jnp.float32),
            pltpu.VMEM(weights.shape, jnp.bfloat16),
            pltpu.VMEM((fine_blocks, 3 * fine_width), jnp.bfloat16),
            pltpu.VMEM((3 * blocks, slots * fine_width), jnp.bfloat16),
            pltpu.VMEM((3, pairs * blocks, fine_blocks), jnp.bfloat16),
            pltpu.VMEM((3, pairs * blocks, fine_blocks), jnp.bfloat16),
            pltpu.VMEM((3, 3 * pairs * blocks, fine_width), jnp.bfloat16),
            pltpu.VMEM((3, 3 * pairs * blocks, fine_width), jnp.bfloat16),
            pltpu.VMEM((rows, LANES), jnp.float32),
            pltpu.VMEM((others, 2 * blocks, LANES), jnp.float32),
            pltpu.VMEM((rows, LANES), jnp.float32),
            dma((4,)), dma((2,)),
            dma((3,)), dma((3,)), dma((3,)), dma((3,)),
            dma((others,)), dma((others,)), dma((others,)), dma((others,)),
        ],
        compiler_params=pltpu.CompilerParams(collective_id=0, has_side_effects=True),
        name="remap",
    )(*operands)
    shift = jnp.swapaxes(delta.reshape(rows // 2, 2, LANES), 0, 1).reshape(2, columns)
    return members + shift[None]


def solution(mesh):
    in_specs = (
        P("mem", None, "tile"),
        P(None, "tile"),
        P(None, "tile"),
        P(None, "tile"),
        P("tile", "mem", None, None, None),
        P("tile", "mem", None),
        P("tile", "mem"),
    )
    out_specs = P("mem", None, "tile")
    return jax.shard_map(shards, mesh=mesh, in_specs=in_specs, out_specs=out_specs, check_vma=False)
```

```python
import functools

import jax
import jax.numpy as jnp
from jax import lax
from jax.experimental import pallas as pl
from jax.experimental.pallas import tpu as pltpu
from jax.sharding import PartitionSpec as P

LANES = 128
MESH = pl.DeviceIdType.MESH


def to_vector(east_part, north_part, longitude, latitude):
    sin_lon, cos_lon = (jnp.sin(longitude), jnp.cos(longitude))
    sin_lat, cos_lat = (jnp.sin(latitude), jnp.cos(latitude))
    first = -sin_lon * east_part - sin_lat * cos_lon * north_part
    second = cos_lon * east_part - sin_lat * sin_lon * north_part
    third = cos_lat * north_part
    return (first, second, third)


def to_wind(first, second, third, longitude, latitude):
    sin_lon, cos_lon = (jnp.sin(longitude), jnp.cos(longitude))
    sin_lat, cos_lat = (jnp.sin(latitude), jnp.cos(latitude))
    east_part = -sin_lon * first + cos_lon * second
    north_part = -sin_lat * cos_lon * first - sin_lat * sin_lon * second + cos_lat * third
    return (east_part, north_part)


def kernel(
    tiles, mems, blocks, slots, fine_blocks, fine_width, member_count,
    src_hbm, cnt_hbm, inc_hbm, ang_hbm, cang_hbm, mem_hbm, w_hbm,
    delta, mem_v,
    src_ref, cnt_ref, inc_v, ang_v, cang_v, w_v,
    cart, picked, req_out, req_in, rows_out, rows_in,
    part, part_in, delta_in,
    load_sem, w_sem, req_send, req_recv, rows_send, rows_recv,
    part_send, part_recv, delta_send, delta_recv,
):
    tile = lax.axis_index("tile")
    mem = lax.axis_index("mem")
    half = tiles // 2
    pairs = (slots - 2) // 2
    halves = fine_width // LANES
    own_rows = 2 * blocks
    wide = pairs * blocks

    barrier = pltpu.get_barrier_semaphore()
    offsets = sorted({1, tiles - 1, half, tiles - half, half + 1, tiles - half - 1})
    for by in offsets:
        pl.semaphore_signal(
            barrier, inc=1, device_id=(mem, lax.rem(tile + by, tiles)), device_id_type=MESH
        )
    for by in range(1, mems):
        pl.semaphore_signal(
            barrier, inc=1, device_id=(lax.rem(mem + by, mems), tile), device_id_type=MESH
        )

    base = pl.multiple_of(mem * own_rows, own_rows)
    loads = [
        pltpu.make_async_copy(src_hbm, src_ref, load_sem.at[0]),
        pltpu.make_async_copy(cnt_hbm, cnt_ref, load_sem.at[1]),
        pltpu.make_async_copy(inc_hbm, inc_v, load_sem.at[2]),
        pltpu.make_async_copy(ang_hbm, ang_v, load_sem.at[3]),
        pltpu.make_async_copy(cang_hbm.at[pl.ds(base, own_rows)], cang_v, load_sem.at[4]),
        pltpu.make_async_copy(mem_hbm, mem_v, load_sem.at[5]),
    ]
    src_load, cnt_load, inc_load, ang_load, cang_load, mem_load = loads
    w_loads = []
    for slot in range(slots):
        depth = pl.ds(slot * fine_width, fine_width)
        w_loads.append(pltpu.make_async_copy(w_hbm.at[:, depth], w_v.at[:, depth], w_sem.at[slot]))
    for load in loads + w_loads:
        load.start()

    row = lax.broadcasted_iota(jnp.int32, (blocks, fine_blocks), 0)
    column = lax.broadcasted_iota(jnp.int32, (blocks, fine_blocks), 1)

    def ids_of(slot):
        ids = jnp.full((blocks, fine_blocks), -1, jnp.int32)
        for block in range(blocks):
            name = jnp.where(slot < cnt_ref[0, block], src_ref[slot, block], -1)
            ids = jnp.where(row == block, name, ids)
        return ids

    def pick(ids, shard):
        return jnp.where(column == ids - shard * fine_blocks, 1.0, 0.0).astype(jnp.bfloat16)

    src_load.wait()
    cnt_load.wait()
    lower = lax.rem(tile + tiles - 1, tiles)
    across = lax.rem(tile + half, tiles)
    beyond = lax.rem(tile + half + 1, tiles)
    own_picks = []
    for pair in range(pairs):
        below_ids = ids_of(2 + 2 * pair)
        across_ids = ids_of(3 + 2 * pair)
        at = slice(pair * blocks, (pair + 1) * blocks)
        req_out[0, at, :] = pick(below_ids, lower)
        req_out[1, at, :] = pick(across_ids, across)
        req_out[2, at, :] = pick(across_ids, beyond)
        own_picks.append(pick(below_ids, tile))
    pl.semaphore_wait(barrier, len(offsets) + mems - 1)

    asked = (lower, across, beyond)
    requests = []
    for flow in range(3):
        requests.append(
            pltpu.make_async_remote_copy(
                src_ref=req_out.at[flow], dst_ref=req_in.at[flow],
                send_sem=req_send.at[flow], recv_sem=req_recv.at[flow],
                device_id=(mem, asked[flow]), device_id_type=MESH,
            )
        )
        requests[-1].start()

    inc_load.wait()
    ang_load.wait()
    step = 32
    for start in range(0, fine_blocks, step):
        for part_at in range(halves):

            def taken(ref, component):
                first_row = start * 2 * halves + 2 * part_at + component
                return ref[pl.ds(first_row, step, stride=2 * halves), :]

            vector = to_vector(taken(inc_v, 0), taken(inc_v, 1), taken(ang_v, 0), taken(ang_v, 1))
            for component in range(3):
                left = component * fine_width + part_at * LANES
                cart[start : start + step, left : left + LANES] = vector[component].astype(jnp.bfloat16)

    served = (
        lax.rem(tile + 1, tiles),
        lax.rem(tile + tiles - half, tiles),
        lax.rem(tile + tiles - half - 1, tiles),
    )
    replies = []
    for flow in range(3):
        requests[flow].wait_recv()
        found = jnp.dot(req_in[flow], cart[...], preferred_element_type=jnp.float32).astype(jnp.bfloat16)
        for component in range(3):
            rows_out[flow, component * wide : (component + 1) * wide, :] = found[
                :, component * fine_width : (component + 1) * fine_width
            ]
        replies.append(
            pltpu.make_async_remote_copy(
                src_ref=rows_out.at[flow], dst_ref=rows_in.at[flow],
                send_sem=rows_send.at[flow], recv_sem=rows_recv.at[flow],
                device_id=(mem, served[flow]), device_id_type=MESH,
            )
        )
        replies[-1].start()

    mem_load.wait()
    part[...] = jnp.sum(mem_v[...], axis=0)
    sums = []
    for by in range(1, mems):
        peer = lax.rem(mem + by, mems)
        sums.append(
            pltpu.make_async_remote_copy(
                src_ref=part.at[pl.ds(pl.multiple_of(peer * own_rows, own_rows), own_rows)],
                dst_ref=part_in.at[by - 1],
                send_sem=part_send.at[by - 1], recv_sem=part_recv.at[by - 1],
                device_id=(peer, tile), device_id_type=MESH,
            )
        )
        sums[-1].start()

    local = jnp.concatenate([pick(ids_of(0), tile), pick(ids_of(1), tile)] + own_picks, axis=0)
    found = jnp.dot(local, cart[...], preferred_element_type=jnp.float32).astype(jnp.bfloat16)
    for order in range(2 + pairs):
        slot = order if order < 2 else 2 * order - 2
        for component in range(3):
            picked[
                component * blocks : (component + 1) * blocks, slot * fine_width : (slot + 1) * fine_width
            ] = found[
                order * blocks : (order + 1) * blocks, component * fine_width : (component + 1) * fine_width
            ]

    cang_load.wait()
    coarse_lon = cang_v[pl.ds(0, blocks, stride=2), :]
    coarse_lat = cang_v[pl.ds(1, blocks, stride=2), :]
    sin_lon, cos_lon = (jnp.sin(coarse_lon), jnp.cos(coarse_lon))
    sin_lat, cos_lat = (jnp.sin(coarse_lat), jnp.cos(coarse_lat))

    owner = lax.rem(lax.broadcasted_iota(jnp.int32, (3 * blocks, LANES), 0), blocks)

    def remap(used, total):
        for block in range(0, blocks, 2):
            product = None
            for slot in used:
                depth = slice(slot * fine_width, (slot + 1) * fine_width)
                both = jnp.concatenate([w_v[block, depth, :], w_v[block + 1, depth, :]], axis=1)
                term = jnp.dot(picked[:, depth], both, preferred_element_type=jnp.float32)
                product = term if product is None else product + term
            width = product.shape[1] // 2
            total = jnp.where(owner == block, total + product[:, :width], total)
            total = jnp.where(owner == block + 1, total + product[:, width:], total)
        return total

    for slot in range(2):
        w_loads[slot].wait()
    vector = remap((0, 1), jnp.zeros((3 * blocks, LANES), jnp.float32))

    for copy in sums:
        copy.wait_recv()
    mean = part[pl.ds(base, own_rows), :]
    for by in range(mems - 1):
        mean = mean + part_in[by]
    mean = mean / member_count

    def arrived(flows, first_slot):
        for flow in flows:
            replies[flow].wait_recv()
        for pair in range(pairs):
            w_loads[first_slot + 2 * pair].wait()
            depth = slice((first_slot + 2 * pair) * fine_width, (first_slot + 2 * pair + 1) * fine_width)
            for component in range(3):
                rows = slice(component * blocks, (component + 1) * blocks)
                came = slice(component * wide + pair * blocks, component * wide + (pair + 1) * blocks)
                terms = [rows_in[flow, came, :] for flow in flows]
                if first_slot == 2:
                    terms.append(picked[rows, depth])
                picked[rows, depth] = terms[0] + terms[1]

    arrived((0,), 2)
    vector = remap(range(2, slots, 2), vector)
    arrived((1, 2), 3)
    vector = remap(range(3, slots, 2), vector)

    first, second, third = (vector[at * blocks : (at + 1) * blocks] for at in range(3))
    east = -sin_lon * first + cos_lon * second
    north = -sin_lat * cos_lon * first - sin_lat * sin_lon * second + cos_lat * third
    mine = pl.ds(base, own_rows)
    delta_in[pl.ds(base, blocks, stride=2), :] = east
    delta_in[pl.ds(base + 1, blocks, stride=2), :] = north
    delta_in[mine, :] = delta_in[mine, :] - mean
    shares = []
    for by in range(1, mems):
        shares.append(
            pltpu.make_async_remote_copy(
                src_ref=delta_in.at[mine], dst_ref=delta_in.at[mine],
                send_sem=delta_send.at[by - 1], recv_sem=delta_recv.at[by - 1],
                device_id=(lax.rem(mem + by, mems), tile), device_id_type=MESH,
            )
        )
        shares[-1].start()
    for copy in shares:
        copy.wait_recv()
    delta[...] = delta_in[...]
    for copy in requests + replies + sums + shares:
        copy.wait_send()


def finish(mem_v, delta, out_hbm, ready, sem):
    copies = []
    for at in range(mem_v.shape[0]):
        ready[at] = mem_v[at] + delta[...]
        copies.append(pltpu.make_async_copy(ready.at[at], out_hbm.at[at], sem.at[at]))
        copies[-1].start()
    for copy in copies:
        copy.wait()


def interleaved(array):
    lead = array.shape[:-2]
    count = array.shape[-1] // LANES
    split = array.reshape(lead + (2, count, LANES))
    return jnp.swapaxes(split, -3, -2).reshape(lead + (2 * count, LANES))


def shards(members, increment, fine_angles, coarse_angles, remap_weights, sources, counts):
    weights = remap_weights[0]
    blocks, slots, fine_width, coarse_width = weights.shape
    fine_blocks = increment.shape[1] // fine_width
    tiles, mems = (lax.axis_size("tile"), lax.axis_size("mem"))
    pairs = (slots - 2) // 2
    weights = weights.reshape(blocks, slots * fine_width, coarse_width)
    columns = coarse_angles.shape[1]
    rows = 2 * columns // LANES
    fine_rows = 2 * increment.shape[1] // LANES
    group = members.shape[0]
    operands = (
        sources[0].T,
        counts,
        interleaved(increment),
        interleaved(fine_angles),
        interleaved(coarse_angles),
        interleaved(members),
        weights,
    )
    any_spec = pl.BlockSpec(memory_space=pl.ANY)
    vmem_spec = pl.BlockSpec(memory_space=pltpu.VMEM)
    dma = pltpu.SemaphoreType.DMA
    others = mems - 1
    delta, held = pl.pallas_call(
        functools.partial(kernel, tiles, mems, blocks, slots, fine_blocks, fine_width, group * mems),
        out_shape=(
            pltpu.VMEM((rows, LANES), jnp.float32),
            pltpu.VMEM((group, rows, LANES), jnp.float32),
        ),
        in_specs=[any_spec] * 7,
        out_specs=(vmem_spec, vmem_spec),
        scratch_shapes=[
            pltpu.SMEM((slots, blocks), jnp.int32),
            pltpu.SMEM((1, blocks), jnp.int32),
            pltpu.VMEM((fine_rows, LANES), jnp.float32),
            pltpu.VMEM((fine_rows, LANES), jnp.float32),
            pltpu.VMEM((2 * blocks, LANES), jnp.float32),
            pltpu.VMEM(weights.shape, jnp.bfloat16),
            pltpu.VMEM((fine_blocks, 3 * fine_width), jnp.bfloat16),
            pltpu.VMEM((3 * blocks, slots * fine_width), jnp.bfloat16),
            pltpu.VMEM((3, pairs * blocks, fine_blocks), jnp.bfloat16),
            pltpu.VMEM((3, pairs * blocks, fine_blocks), jnp.bfloat16),
            pltpu.VMEM((3, 3 * pairs * blocks, fine_width), jnp.bfloat16),
            pltpu.VMEM((3, 3 * pairs * blocks, fine_width), jnp.bfloat16),
            pltpu.VMEM((rows, LANES), jnp.float32),
            pltpu.VMEM((others, 2 * blocks, LANES), jnp.float32),
            pltpu.VMEM((rows, LANES), jnp.float32),
            dma((6,)), dma((slots,)),
            dma((3,)), dma((3,)), dma((3,)), dma((3,)),
            dma((others,)), dma((others,)), dma((others,)), dma((others,)),
        ],
        compiler_params=pltpu.CompilerParams(collective_id=0, has_side_effects=True),
        name="remap",
    )(*operands)
    recentered = pl.pallas_call(
        finish,
        out_shape=jax.ShapeDtypeStruct((group, rows, LANES), jnp.float32),
        in_specs=[vmem_spec, vmem_spec],
        out_specs=any_spec,
        scratch_shapes=[pltpu.VMEM((group, rows, LANES), jnp.float32), dma((group,))],
        name="recenter",
    )(*(pltpu.with_memory_space_constraint(array, pltpu.VMEM) for array in (held, delta)))
    split = recentered.reshape(group, rows // 2, 2, LANES)
    return jnp.swapaxes(split, 1, 2).reshape(members.shape)


def solution(mesh):
    in_specs = (
        P("mem", None, "tile"),
        P(None, "tile"),
        P(None, "tile"),
        P(None, "tile"),
        P("tile", "mem", None, None, None),
        P("tile", "mem", None),
        P("tile", "mem"),
    )
    out_specs = P("mem", None, "tile")
    return jax.shard_map(shards, mesh=mesh, in_specs=in_specs, out_specs=out_specs, check_vma=False)
```

```python
import functools

import jax
import jax.numpy as jnp
from jax import lax
from jax.experimental import pallas as pl
from jax.experimental.pallas import tpu as pltpu
from jax.sharding import PartitionSpec as P

LANES = 128
MESH = pl.DeviceIdType.MESH


def to_vector(east_part, north_part, longitude, latitude):
    sin_lon, cos_lon = (jnp.sin(longitude), jnp.cos(longitude))
    sin_lat, cos_lat = (jnp.sin(latitude), jnp.cos(latitude))
    first = -sin_lon * east_part - sin_lat * cos_lon * north_part
    second = cos_lon * east_part - sin_lat * sin_lon * north_part
    third = cos_lat * north_part
    return (first, second, third)


def to_wind(first, second, third, longitude, latitude):
    sin_lon, cos_lon = (jnp.sin(longitude), jnp.cos(longitude))
    sin_lat, cos_lat = (jnp.sin(latitude), jnp.cos(latitude))
    east_part = -sin_lon * first + cos_lon * second
    north_part = -sin_lat * cos_lon * first - sin_lat * sin_lon * second + cos_lat * third
    return (east_part, north_part)


def kernel(
    tiles, mems, blocks, slots, fine_blocks, fine_width, member_count,
    src_hbm, cnt_hbm, inc_hbm, ang_hbm, cang_hbm, mem_hbm, w_hbm,
    delta, mem_v,
    src_ref, cnt_ref, inc_v, ang_v, cang_v, w_v,
    cart, picked, req_out, req_in, rows_out, rows_in,
    part, part_in, delta_in, share,
    load_sem, w_sem, req_send, req_recv, rows_send, rows_recv,
    part_send, part_recv, delta_send, delta_recv,
):
    tile = lax.axis_index("tile")
    mem = lax.axis_index("mem")
    half = tiles // 2
    pairs = (slots - 2) // 2
    halves = fine_width // LANES
    own_rows = 2 * blocks
    wide = pairs * blocks

    barrier = pltpu.get_barrier_semaphore()
    offsets = sorted({1, tiles - 1, half, tiles - half, half + 1, tiles - half - 1})
    for by in offsets:
        pl.semaphore_signal(
            barrier, inc=1, device_id=(mem, lax.rem(tile + by, tiles)), device_id_type=MESH
        )
    for by in range(1, mems):
        pl.semaphore_signal(
            barrier, inc=1, device_id=(lax.rem(mem + by, mems), tile), device_id_type=MESH
        )

    base = pl.multiple_of(mem * own_rows, own_rows)
    loads = [
        pltpu.make_async_copy(src_hbm, src_ref, load_sem.at[0]),
        pltpu.make_async_copy(cnt_hbm, cnt_ref, load_sem.at[1]),
        pltpu.make_async_copy(inc_hbm, inc_v, load_sem.at[2]),
        pltpu.make_async_copy(ang_hbm, ang_v, load_sem.at[3]),
        pltpu.make_async_copy(cang_hbm.at[pl.ds(base, own_rows)], cang_v, load_sem.at[4]),
        pltpu.make_async_copy(mem_hbm, mem_v, load_sem.at[5]),
    ]
    src_load, cnt_load, inc_load, ang_load, cang_load, mem_load = loads
    w_loads = []
    for slot in range(slots):
        depth = pl.ds(slot * fine_width, fine_width)
        w_loads.append(pltpu.make_async_copy(w_hbm.at[:, depth], w_v.at[:, depth], w_sem.at[slot]))
    for load in loads + w_loads:
        load.start()

    row = lax.broadcasted_iota(jnp.int32, (blocks, fine_blocks), 0)
    column = lax.broadcasted_iota(jnp.int32, (blocks, fine_blocks), 1)

    def ids_of(slot):
        ids = jnp.full((blocks, fine_blocks), -1, jnp.int32)
        for block in range(blocks):
            name = jnp.where(slot < cnt_ref[0, block], src_ref[slot, block], -1)
            ids = jnp.where(row == block, name, ids)
        return ids

    def pick(ids, shard):
        return jnp.where(column == ids - shard * fine_blocks, 1.0, 0.0).astype(jnp.bfloat16)

    src_load.wait()
    cnt_load.wait()
    lower = lax.rem(tile + tiles - 1, tiles)
    across = lax.rem(tile + half, tiles)
    beyond = lax.rem(tile + half + 1, tiles)
    own_picks = []
    for pair in range(pairs):
        below_ids = ids_of(2 + 2 * pair)
        across_ids = ids_of(3 + 2 * pair)
        at = slice(pair * blocks, (pair + 1) * blocks)
        req_out[0, at, :] = pick(below_ids, lower)
        req_out[1, at, :] = pick(across_ids, across)
        req_out[2, at, :] = pick(across_ids, beyond)
        own_picks.append(pick(below_ids, tile))
    pl.semaphore_wait(barrier, len(offsets) + mems - 1)

    asked = (lower, across, beyond)
    requests = []
    for flow in range(3):
        requests.append(
            pltpu.make_async_remote_copy(
                src_ref=req_out.at[flow], dst_ref=req_in.at[flow],
                send_sem=req_send.at[flow], recv_sem=req_recv.at[flow],
                device_id=(mem, asked[flow]), device_id_type=MESH,
            )
        )
        requests[-1].start()

    inc_load.wait()
    ang_load.wait()
    step = 32
    for start in range(0, fine_blocks, step):
        for part_at in range(halves):

            def taken(ref, component):
                first_row = start * 2 * halves + 2 * part_at + component
                return ref[pl.ds(first_row, step, stride=2 * halves), :]

            vector = to_vector(taken(inc_v, 0), taken(inc_v, 1), taken(ang_v, 0), taken(ang_v, 1))
            for component in range(3):
                left = component * fine_width + part_at * LANES
                cart[start : start + step, left : left + LANES] = vector[component].astype(jnp.bfloat16)

    served = (
        lax.rem(tile + 1, tiles),
        lax.rem(tile + tiles - half, tiles),
        lax.rem(tile + tiles - half - 1, tiles),
    )
    replies = []
    for flow in range(3):
        requests[flow].wait_recv()
        found = jnp.dot(req_in[flow], cart[...], preferred_element_type=jnp.float32).astype(jnp.bfloat16)
        for component in range(3):
            rows_out[flow, component * wide : (component + 1) * wide, :] = found[
                :, component * fine_width : (component + 1) * fine_width
            ]
        replies.append(
            pltpu.make_async_remote_copy(
                src_ref=rows_out.at[flow], dst_ref=rows_in.at[flow],
                send_sem=rows_send.at[flow], recv_sem=rows_recv.at[flow],
                device_id=(mem, served[flow]), device_id_type=MESH,
            )
        )
        replies[-1].start()

    mem_load.wait()
    part[...] = jnp.sum(mem_v[...], axis=0)
    sums = []
    for by in range(1, mems):
        peer = lax.rem(mem + by, mems)
        sums.append(
            pltpu.make_async_remote_copy(
                src_ref=part.at[pl.ds(pl.multiple_of(peer * own_rows, own_rows), own_rows)],
                dst_ref=part_in.at[by - 1],
                send_sem=part_send.at[by - 1], recv_sem=part_recv.at[by - 1],
                device_id=(peer, tile), device_id_type=MESH,
            )
        )
        sums[-1].start()

    local = jnp.concatenate([pick(ids_of(0), tile), pick(ids_of(1), tile)] + own_picks, axis=0)
    found = jnp.dot(local, cart[...], preferred_element_type=jnp.float32).astype(jnp.bfloat16)
    for order in range(2 + pairs):
        slot = order if order < 2 else 2 * order - 2
        for component in range(3):
            picked[
                component * blocks : (component + 1) * blocks, slot * fine_width : (slot + 1) * fine_width
            ] = found[
                order * blocks : (order + 1) * blocks, component * fine_width : (component + 1) * fine_width
            ]

    cang_load.wait()
    coarse_lon = cang_v[pl.ds(0, blocks, stride=2), :]
    coarse_lat = cang_v[pl.ds(1, blocks, stride=2), :]
    sin_lon, cos_lon = (jnp.sin(coarse_lon), jnp.cos(coarse_lon))
    sin_lat, cos_lat = (jnp.sin(coarse_lat), jnp.cos(coarse_lat))

    owner = lax.rem(lax.broadcasted_iota(jnp.int32, (3 * blocks, LANES), 0), blocks)

    def remap(used, total):
        for block in range(0, blocks, 2):
            product = None
            for slot in used:
                depth = slice(slot * fine_width, (slot + 1) * fine_width)
                both = jnp.concatenate([w_v[block, depth, :], w_v[block + 1, depth, :]], axis=1)
                term = jnp.dot(picked[:, depth], both, preferred_element_type=jnp.float32)
                product = term if product is None else product + term
            width = product.shape[1] // 2
            total = jnp.where(owner == block, total + product[:, :width], total)
            total = jnp.where(owner == block + 1, total + product[:, width:], total)
        return total

    for slot in range(2):
        w_loads[slot].wait()
    vector = remap((0, 1), jnp.zeros((3 * blocks, LANES), jnp.float32))

    for copy in sums:
        copy.wait_recv()
    mean = part[pl.ds(base, own_rows), :]
    for by in range(mems - 1):
        mean = mean + part_in[by]
    mean = mean / member_count

    def arrived(flows, first_slot):
        for flow in flows:
            replies[flow].wait_recv()
        for pair in range(pairs):
            w_loads[first_slot + 2 * pair].wait()
            depth = slice((first_slot + 2 * pair) * fine_width, (first_slot + 2 * pair + 1) * fine_width)
            for component in range(3):
                rows = slice(component * blocks, (component + 1) * blocks)
                came = slice(component * wide + pair * blocks, component * wide + (pair + 1) * blocks)
                terms = [rows_in[flow, came, :] for flow in flows]
                if first_slot == 2:
                    terms.append(picked[rows, depth])
                picked[rows, depth] = terms[0] + terms[1]

    arrived((0,), 2)
    vector = remap(range(2, slots, 2), vector)
    arrived((1, 2), 3)
    vector = remap(range(3, slots, 2), vector)

    first, second, third = (vector[at * blocks : (at + 1) * blocks] for at in range(3))
    east = -sin_lon * first + cos_lon * second
    north = -sin_lat * cos_lon * first - sin_lat * sin_lon * second + cos_lat * third
    mine = pl.ds(base, own_rows)
    delta_in[pl.ds(base, blocks, stride=2), :] = east
    delta_in[pl.ds(base + 1, blocks, stride=2), :] = north
    delta[mine, :] = delta_in[mine, :] - mean
    share[mine, :] = delta[mine, :].astype(jnp.bfloat16)
    shares = []
    for by in range(1, mems):
        shares.append(
            pltpu.make_async_remote_copy(
                src_ref=share.at[mine], dst_ref=share.at[mine],
                send_sem=delta_send.at[by - 1], recv_sem=delta_recv.at[by - 1],
                device_id=(lax.rem(mem + by, mems), tile), device_id_type=MESH,
            )
        )
        shares[-1].start()
    for by in range(1, mems):
        shares[by - 1].wait_recv()
        came = pl.ds(pl.multiple_of(lax.rem(mem + mems - by, mems) * own_rows, own_rows), own_rows)
        delta[came, :] = share[came, :].astype(jnp.float32)
    for copy in requests + replies + sums + shares:
        copy.wait_send()


def finish(mem_v, delta, out_hbm, ready, sem):
    copies = []
    for at in range(mem_v.shape[0]):
        ready[at] = mem_v[at] + delta[...]
        copies.append(pltpu.make_async_copy(ready.at[at], out_hbm.at[at], sem.at[at]))
        copies[-1].start()
    for copy in copies:
        copy.wait()


def interleaved(array):
    lead = array.shape[:-2]
    count = array.shape[-1] // LANES
    split = array.reshape(lead + (2, count, LANES))
    return jnp.swapaxes(split, -3, -2).reshape(lead + (2 * count, LANES))


def shards(members, increment, fine_angles, coarse_angles, remap_weights, sources, counts):
    weights = remap_weights[0]
    blocks, slots, fine_width, coarse_width = weights.shape
    fine_blocks = increment.shape[1] // fine_width
    tiles, mems = (lax.axis_size("tile"), lax.axis_size("mem"))
    pairs = (slots - 2) // 2
    weights = weights.reshape(blocks, slots * fine_width, coarse_width)
    columns = coarse_angles.shape[1]
    rows = 2 * columns // LANES
    fine_rows = 2 * increment.shape[1] // LANES
    group = members.shape[0]
    operands = (
        sources[0].T,
        counts,
        interleaved(increment),
        interleaved(fine_angles),
        interleaved(coarse_angles),
        interleaved(members),
        weights,
    )
    any_spec = pl.BlockSpec(memory_space=pl.ANY)
    vmem_spec = pl.BlockSpec(memory_space=pltpu.VMEM)
    dma = pltpu.SemaphoreType.DMA
    others = mems - 1
    delta, held = pl.pallas_call(
        functools.partial(kernel, tiles, mems, blocks, slots, fine_blocks, fine_width, group * mems),
        out_shape=(
            pltpu.VMEM((rows, LANES), jnp.float32),
            pltpu.VMEM((group, rows, LANES), jnp.float32),
        ),
        in_specs=[any_spec] * 7,
        out_specs=(vmem_spec, vmem_spec),
        scratch_shapes=[
            pltpu.SMEM((slots, blocks), jnp.int32),
            pltpu.SMEM((1, blocks), jnp.int32),
            pltpu.VMEM((fine_rows, LANES), jnp.float32),
            pltpu.VMEM((fine_rows, LANES), jnp.float32),
            pltpu.VMEM((2 * blocks, LANES), jnp.float32),
            pltpu.VMEM(weights.shape, jnp.bfloat16),
            pltpu.VMEM((fine_blocks, 3 * fine_width), jnp.bfloat16),
            pltpu.VMEM((3 * blocks, slots * fine_width), jnp.bfloat16),
            pltpu.VMEM((3, pairs * blocks, fine_blocks), jnp.bfloat16),
            pltpu.VMEM((3, pairs * blocks, fine_blocks), jnp.bfloat16),
            pltpu.VMEM((3, 3 * pairs * blocks, fine_width), jnp.bfloat16),
            pltpu.VMEM((3, 3 * pairs * blocks, fine_width), jnp.bfloat16),
            pltpu.VMEM((rows, LANES), jnp.float32),
            pltpu.VMEM((others, 2 * blocks, LANES), jnp.float32),
            pltpu.VMEM((rows, LANES), jnp.float32),
            pltpu.VMEM((rows, LANES), jnp.bfloat16),
            dma((6,)), dma((slots,)),
            dma((3,)), dma((3,)), dma((3,)), dma((3,)),
            dma((others,)), dma((others,)), dma((others,)), dma((others,)),
        ],
        compiler_params=pltpu.CompilerParams(collective_id=0, has_side_effects=True),
        name="remap",
    )(*operands)
    recentered = pl.pallas_call(
        finish,
        out_shape=jax.ShapeDtypeStruct((group, rows, LANES), jnp.float32),
        in_specs=[vmem_spec, vmem_spec],
        out_specs=any_spec,
        scratch_shapes=[pltpu.VMEM((group, rows, LANES), jnp.float32), dma((group,))],
        name="recenter",
    )(*(pltpu.with_memory_space_constraint(array, pltpu.VMEM) for array in (held, delta)))
    split = recentered.reshape(group, rows // 2, 2, LANES)
    return jnp.swapaxes(split, 1, 2).reshape(members.shape)


def solution(mesh):
    in_specs = (
        P("mem", None, "tile"),
        P(None, "tile"),
        P(None, "tile"),
        P(None, "tile"),
        P("tile", "mem", None, None, None),
        P("tile", "mem", None),
        P("tile", "mem"),
    )
    out_specs = P("mem", None, "tile")
    return jax.shard_map(shards, mesh=mesh, in_specs=in_specs, out_specs=out_specs, check_vma=False)
```

```python
import functools

import jax
import jax.numpy as jnp
from jax import lax
from jax.experimental import pallas as pl
from jax.experimental.pallas import tpu as pltpu
from jax.sharding import PartitionSpec as P

LANES = 128
MESH = pl.DeviceIdType.MESH


def to_vector(east_part, north_part, longitude, latitude):
    sin_lon, cos_lon = (jnp.sin(longitude), jnp.cos(longitude))
    sin_lat, cos_lat = (jnp.sin(latitude), jnp.cos(latitude))
    first = -sin_lon * east_part - sin_lat * cos_lon * north_part
    second = cos_lon * east_part - sin_lat * sin_lon * north_part
    third = cos_lat * north_part
    return (first, second, third)


def to_wind(first, second, third, longitude, latitude):
    sin_lon, cos_lon = (jnp.sin(longitude), jnp.cos(longitude))
    sin_lat, cos_lat = (jnp.sin(latitude), jnp.cos(latitude))
    east_part = -sin_lon * first + cos_lon * second
    north_part = -sin_lat * cos_lon * first - sin_lat * sin_lon * second + cos_lat * third
    return (east_part, north_part)


def kernel(
    tiles, mems, blocks, slots, fine_blocks, fine_width, member_count,
    src_hbm, cnt_hbm, inc_hbm, ang_hbm, cang_hbm, mem_hbm, w_hbm,
    delta, mem_v,
    src_ref, cnt_ref, inc_v, ang_v, cang_v, w_v,
    cart, picked, req_out, req_in, rows_out, rows_in,
    part, part_in, delta_in, share,
    load_sem, w_sem, req_send, req_recv, rows_send, rows_recv,
    part_send, part_recv, delta_send, delta_recv,
):
    tile = lax.axis_index("tile")
    mem = lax.axis_index("mem")
    half = tiles // 2
    pairs = (slots - 2) // 2
    halves = fine_width // LANES
    own_rows = 2 * blocks
    wide = pairs * blocks

    src_load = pltpu.make_async_copy(src_hbm, src_ref, load_sem.at[0])
    cnt_load = pltpu.make_async_copy(cnt_hbm, cnt_ref, load_sem.at[1])
    src_load.start()
    cnt_load.start()
    barrier = pltpu.get_barrier_semaphore()
    offsets = sorted({1, tiles - 1, half, tiles - half, half + 1, tiles - half - 1})
    for by in offsets:
        pl.semaphore_signal(
            barrier, inc=1, device_id=(mem, lax.rem(tile + by, tiles)), device_id_type=MESH
        )
    for by in range(1, mems):
        pl.semaphore_signal(
            barrier, inc=1, device_id=(lax.rem(mem + by, mems), tile), device_id_type=MESH
        )

    base = pl.multiple_of(mem * own_rows, own_rows)
    loads = [
        pltpu.make_async_copy(inc_hbm, inc_v, load_sem.at[2]),
        pltpu.make_async_copy(ang_hbm, ang_v, load_sem.at[3]),
        pltpu.make_async_copy(cang_hbm.at[pl.ds(base, own_rows)], cang_v, load_sem.at[4]),
        pltpu.make_async_copy(mem_hbm, mem_v, load_sem.at[5]),
    ]
    inc_load, ang_load, cang_load, mem_load = loads
    w_loads = []
    for slot in range(slots):
        depth = pl.ds(slot * fine_width, fine_width)
        w_loads.append(pltpu.make_async_copy(w_hbm.at[:, depth], w_v.at[:, depth], w_sem.at[slot]))
    for load in loads + w_loads:
        load.start()

    row = lax.broadcasted_iota(jnp.int32, (blocks, fine_blocks), 0)
    column = lax.broadcasted_iota(jnp.int32, (blocks, fine_blocks), 1)

    def ids_of(slot):
        ids = jnp.full((blocks, fine_blocks), -1, jnp.int32)
        for block in range(blocks):
            name = jnp.where(slot < cnt_ref[0, block], src_ref[slot, block], -1)
            ids = jnp.where(row == block, name, ids)
        return ids

    def pick(ids, shard):
        return jnp.where(column == ids - shard * fine_blocks, 1.0, 0.0).astype(jnp.bfloat16)

    src_load.wait()
    cnt_load.wait()
    lower = lax.rem(tile + tiles - 1, tiles)
    across = lax.rem(tile + half, tiles)
    beyond = lax.rem(tile + half + 1, tiles)
    own_picks = []
    for pair in range(pairs):
        below_ids = ids_of(2 + 2 * pair)
        across_ids = ids_of(3 + 2 * pair)
        at = slice(pair * blocks, (pair + 1) * blocks)
        req_out[0, at, :] = pick(below_ids, lower)
        req_out[1, at, :] = pick(across_ids, across)
        req_out[2, at, :] = pick(across_ids, beyond)
        own_picks.append(pick(below_ids, tile))
    pl.semaphore_wait(barrier, len(offsets) + mems - 1)

    asked = (lower, across, beyond)
    requests = []
    for flow in range(3):
        requests.append(
            pltpu.make_async_remote_copy(
                src_ref=req_out.at[flow], dst_ref=req_in.at[flow],
                send_sem=req_send.at[flow], recv_sem=req_recv.at[flow],
                device_id=(mem, asked[flow]), device_id_type=MESH,
            )
        )
        requests[-1].start()

    inc_load.wait()
    ang_load.wait()
    step = 32
    for start in range(0, fine_blocks, step):
        for part_at in range(halves):

            def taken(ref, component):
                first_row = start * 2 * halves + 2 * part_at + component
                return ref[pl.ds(first_row, step, stride=2 * halves), :]

            vector = to_vector(taken(inc_v, 0), taken(inc_v, 1), taken(ang_v, 0), taken(ang_v, 1))
            for component in range(3):
                left = component * fine_width + part_at * LANES
                cart[start : start + step, left : left + LANES] = vector[component].astype(jnp.bfloat16)

    served = (
        lax.rem(tile + 1, tiles),
        lax.rem(tile + tiles - half, tiles),
        lax.rem(tile + tiles - half - 1, tiles),
    )
    replies = []
    for flow in range(3):
        requests[flow].wait_recv()
        found = jnp.dot(req_in[flow], cart[...], preferred_element_type=jnp.float32).astype(jnp.bfloat16)
        for component in range(3):
            rows_out[flow, component * wide : (component + 1) * wide, :] = found[
                :, component * fine_width : (component + 1) * fine_width
            ]
        replies.append(
            pltpu.make_async_remote_copy(
                src_ref=rows_out.at[flow], dst_ref=rows_in.at[flow],
                send_sem=rows_send.at[flow], recv_sem=rows_recv.at[flow],
                device_id=(mem, served[flow]), device_id_type=MESH,
            )
        )
        replies[-1].start()

    mem_load.wait()
    part[...] = jnp.sum(mem_v[...], axis=0)
    sums = []
    for by in range(1, mems):
        peer = lax.rem(mem + by, mems)
        sums.append(
            pltpu.make_async_remote_copy(
                src_ref=part.at[pl.ds(pl.multiple_of(peer * own_rows, own_rows), own_rows)],
                dst_ref=part_in.at[by - 1],
                send_sem=part_send.at[by - 1], recv_sem=part_recv.at[by - 1],
                device_id=(peer, tile), device_id_type=MESH,
            )
        )
        sums[-1].start()

    local = jnp.concatenate([pick(ids_of(0), tile), pick(ids_of(1), tile)] + own_picks, axis=0)
    found = jnp.dot(local, cart[...], preferred_element_type=jnp.float32).astype(jnp.bfloat16)
    for order in range(2 + pairs):
        slot = order if order < 2 else 2 * order - 2
        for component in range(3):
            picked[
                component * blocks : (component + 1) * blocks, slot * fine_width : (slot + 1) * fine_width
            ] = found[
                order * blocks : (order + 1) * blocks, component * fine_width : (component + 1) * fine_width
            ]

    cang_load.wait()
    coarse_lon = cang_v[pl.ds(0, blocks, stride=2), :]
    coarse_lat = cang_v[pl.ds(1, blocks, stride=2), :]
    sin_lon, cos_lon = (jnp.sin(coarse_lon), jnp.cos(coarse_lon))
    sin_lat, cos_lat = (jnp.sin(coarse_lat), jnp.cos(coarse_lat))

    owner = lax.rem(lax.broadcasted_iota(jnp.int32, (3 * blocks, LANES), 0), blocks)

    def remap(used, total):
        for block in range(0, blocks, 2):
            product = None
            for slot in used:
                depth = slice(slot * fine_width, (slot + 1) * fine_width)
                both = jnp.concatenate([w_v[block, depth, :], w_v[block + 1, depth, :]], axis=1)
                term = jnp.dot(picked[:, depth], both, preferred_element_type=jnp.float32)
                product = term if product is None else product + term
            width = product.shape[1] // 2
            total = jnp.where(owner == block, total + product[:, :width], total)
            total = jnp.where(owner == block + 1, total + product[:, width:], total)
        return total

    for slot in range(2):
        w_loads[slot].wait()
    vector = remap((0, 1), jnp.zeros((3 * blocks, LANES), jnp.float32))

    for copy in sums:
        copy.wait_recv()
    mean = part[pl.ds(base, own_rows), :]
    for by in range(mems - 1):
        mean = mean + part_in[by]
    mean = mean / member_count

    def arrived(flows, first_slot):
        for flow in flows:
            replies[flow].wait_recv()
        for pair in range(pairs):
            w_loads[first_slot + 2 * pair].wait()
            depth = slice((first_slot + 2 * pair) * fine_width, (first_slot + 2 * pair + 1) * fine_width)
            for component in range(3):
                rows = slice(component * blocks, (component + 1) * blocks)
                came = slice(component * wide + pair * blocks, component * wide + (pair + 1) * blocks)
                terms = [rows_in[flow, came, :] for flow in flows]
                if first_slot == 2:
                    terms.append(picked[rows, depth])
                picked[rows, depth] = terms[0] + terms[1]

    arrived((0,), 2)
    vector = remap(range(2, slots, 2), vector)
    arrived((1, 2), 3)
    vector = remap(range(3, slots, 2), vector)

    first, second, third = (vector[at * blocks : (at + 1) * blocks] for at in range(3))
    east = -sin_lon * first + cos_lon * second
    north = -sin_lat * cos_lon * first - sin_lat * sin_lon * second + cos_lat * third
    mine = pl.ds(base, own_rows)
    delta_in[pl.ds(base, blocks, stride=2), :] = east
    delta_in[pl.ds(base + 1, blocks, stride=2), :] = north
    delta[mine, :] = delta_in[mine, :] - mean
    share[mine, :] = delta[mine, :].astype(jnp.bfloat16)
    shares = []
    for by in range(1, mems):
        shares.append(
            pltpu.make_async_remote_copy(
                src_ref=share.at[mine], dst_ref=share.at[mine],
                send_sem=delta_send.at[by - 1], recv_sem=delta_recv.at[by - 1],
                device_id=(lax.rem(mem + by, mems), tile), device_id_type=MESH,
            )
        )
        shares[-1].start()
    for by in range(1, mems):
        shares[by - 1].wait_recv()
        came = pl.ds(pl.multiple_of(lax.rem(mem + mems - by, mems) * own_rows, own_rows), own_rows)
        delta[came, :] = share[came, :].astype(jnp.float32)
    for copy in requests + replies + sums + shares:
        copy.wait_send()


def finish(mem_v, delta, out_hbm, ready, sem):
    copies = []
    for at in range(mem_v.shape[0]):
        ready[at] = mem_v[at] + delta[...]
        copies.append(pltpu.make_async_copy(ready.at[at], out_hbm.at[at], sem.at[at]))
        copies[-1].start()
    for copy in copies:
        copy.wait()


def interleaved(array):
    lead = array.shape[:-2]
    count = array.shape[-1] // LANES
    split = array.reshape(lead + (2, count, LANES))
    return jnp.swapaxes(split, -3, -2).reshape(lead + (2 * count, LANES))


def shards(members, increment, fine_angles, coarse_angles, remap_weights, sources, counts):
    weights = remap_weights[0]
    blocks, slots, fine_width, coarse_width = weights.shape
    fine_blocks = increment.shape[1] // fine_width
    tiles, mems = (lax.axis_size("tile"), lax.axis_size("mem"))
    pairs = (slots - 2) // 2
    weights = weights.reshape(blocks, slots * fine_width, coarse_width)
    columns = coarse_angles.shape[1]
    rows = 2 * columns // LANES
    fine_rows = 2 * increment.shape[1] // LANES
    group = members.shape[0]
    operands = (
        sources[0].T,
        counts,
        interleaved(increment),
        interleaved(fine_angles),
        interleaved(coarse_angles),
        interleaved(members),
        weights,
    )
    any_spec = pl.BlockSpec(memory_space=pl.ANY)
    vmem_spec = pl.BlockSpec(memory_space=pltpu.VMEM)
    dma = pltpu.SemaphoreType.DMA
    others = mems - 1
    delta, held = pl.pallas_call(
        functools.partial(kernel, tiles, mems, blocks, slots, fine_blocks, fine_width, group * mems),
        out_shape=(
            pltpu.VMEM((rows, LANES), jnp.float32),
            pltpu.VMEM((group, rows, LANES), jnp.float32),
        ),
        in_specs=[any_spec] * 7,
        out_specs=(vmem_spec, vmem_spec),
        scratch_shapes=[
            pltpu.SMEM((slots, blocks), jnp.int32),
            pltpu.SMEM((1, blocks), jnp.int32),
            pltpu.VMEM((fine_rows, LANES), jnp.float32),
            pltpu.VMEM((fine_rows, LANES), jnp.float32),
            pltpu.VMEM((2 * blocks, LANES), jnp.float32),
            pltpu.VMEM(weights.shape, jnp.bfloat16),
            pltpu.VMEM((fine_blocks, 3 * fine_width), jnp.bfloat16),
            pltpu.VMEM((3 * blocks, slots * fine_width), jnp.bfloat16),
            pltpu.VMEM((3, pairs * blocks, fine_blocks), jnp.bfloat16),
            pltpu.VMEM((3, pairs * blocks, fine_blocks), jnp.bfloat16),
            pltpu.VMEM((3, 3 * pairs * blocks, fine_width), jnp.bfloat16),
            pltpu.VMEM((3, 3 * pairs * blocks, fine_width), jnp.bfloat16),
            pltpu.VMEM((rows, LANES), jnp.float32),
            pltpu.VMEM((others, 2 * blocks, LANES), jnp.float32),
            pltpu.VMEM((rows, LANES), jnp.float32),
            pltpu.VMEM((rows, LANES), jnp.bfloat16),
            dma((6,)), dma((slots,)),
            dma((3,)), dma((3,)), dma((3,)), dma((3,)),
            dma((others,)), dma((others,)), dma((others,)), dma((others,)),
        ],
        compiler_params=pltpu.CompilerParams(collective_id=0, has_side_effects=True),
        name="remap",
    )(*operands)
    recentered = pl.pallas_call(
        finish,
        out_shape=jax.ShapeDtypeStruct((group, rows, LANES), jnp.float32),
        in_specs=[vmem_spec, vmem_spec],
        out_specs=any_spec,
        scratch_shapes=[pltpu.VMEM((group, rows, LANES), jnp.float32), dma((group,))],
        name="recenter",
    )(*(pltpu.with_memory_space_constraint(array, pltpu.VMEM) for array in (held, delta)))
    split = recentered.reshape(group, rows // 2, 2, LANES)
    return jnp.swapaxes(split, 1, 2).reshape(members.shape)


def solution(mesh):
    in_specs = (
        P("mem", None, "tile"),
        P(None, "tile"),
        P(None, "tile"),
        P(None, "tile"),
        P("tile", "mem", None, None, None),
        P("tile", "mem", None),
        P("tile", "mem"),
    )
    out_specs = P("mem", None, "tile")
    return jax.shard_map(shards, mesh=mesh, in_specs=in_specs, out_specs=out_specs, check_vma=False)
```
